32 devices in a mesh: dp: 4 (over x, core), expert: 8 (over z, y).
Axes of the slice: x: 2, y: 2, z: 4, core: 2. Of those that a mesh axis runs over, the one named last changes fastest.
Arguments:
- tokens: bfloat16 [320, 4096], P('expert', 'dp'), may hold values from -6 to 6
- expert_ids: int32 [320, 8], P('expert'), may hold values from 0 to 15, all different within a row; in each aligned block of 320 rows (0 to 319, 320 to 639, ...) at most 240 rows name the same one
- routing_weights: bfloat16 [320, 8], P('expert'), may hold values from 0.049804688 to 0.29882812
- gate_weight: bfloat16 [16, 768, 4096], P('expert', None, 'dp'), may hold values from -0.09375 to 0.09375
- up_weight: bfloat16 [16, 768, 4096], P('expert', None, 'dp'), may hold values from -0.09375 to 0.09375
- down_weight: bfloat16 [16, 768, 4096], P('expert', None, 'dp'), may hold values from -0.21875 to 0.21875
- out_grad: bfloat16 [320, 4096], P('expert', 'dp'), may hold values from -1.5 to 1.5
Outputs:
- layer_out: bfloat16 [320, 4096], P('expert', 'dp')
- tokens_grad: bfloat16 [320, 4096], P('expert', 'dp')
- routing_grad: float32 [320, 8], P('expert')
- gate_weight_grad: bfloat16 [16, 768, 4096], P('expert', None, 'dp')
- up_weight_grad: bfloat16 [16, 768, 4096], P('expert', None, 'dp')
- down_weight_grad: bfloat16 [16, 768, 4096], P('expert', None, 'dp')
The draws below stay inside these ranges and needn't reach their ends.
Inputs may be any that keep to these rules, and one draw needn't show every extreme that they name: `expert_ids`: each row names 8 different experts. No expert is named by more than 240 rows, a bound that some block reaches.
All inputs are finite; a program needn't handle non-finite values.
Results may differ from the reference program's by a relative error of at most 0.02.
Values may be sent and summed in bfloat16 or wider, within the bound.
A program may use at most 128 MiB of HBM per device.

```python
import math
import jax
import jax.numpy as jnp
import numpy as np
from jax import lax

D = 4096
FF = 768
TOP = 8
EXP_DEV = 2
EXPERTS = 16
TOKENS = 320
CAP = 240
N_DP = 4
N_EXPERT = 8


def shard_levels(own_key, extent, pieces, smallest, largest):
    loudness = 1.0
    for dim, blocks in pieces:
        steps = jax.random.uniform(jax.random.fold_in(jax.random.fold_in(own_key, 6), dim), (blocks,), jnp.float32, smallest / len(pieces), largest / len(pieces))
        loudness = loudness * jnp.repeat(jnp.exp(steps), extent[dim] // blocks).reshape((-1,) + (1,) * (len(extent) - 1 - dim))
    return loudness


def deal_out(own_key, own, number, rows, count, top, most, slope):
    order = jax.random.permutation(own_key, count)
    crowded, ordinary = shares(count, rows * top, most, slope, True), shares(count, rows * top, most, slope, False)
    places = jnp.arange(count)

    def named(lengths, offset_by):
        used = int((lengths > 0).sum())
        fixed = max(1, used // 4)
        shifted = fixed + (places - fixed + offset_by * (used - fixed)) % max(1, count - fixed)
        return jnp.zeros((count,), jnp.int32).at[order[jnp.where(places < fixed, places, shifted)]].set(jnp.asarray(lengths, jnp.int32))

    lengths = jnp.where(number % 4 == 0, named(crowded, number // 4), named(ordinary, number - number // 4 - 1))
    mixed = jax.random.permutation(jax.random.fold_in(own, 3), count)
    giver, receiver = mixed[0:count // 2 * 2:2], mixed[1:count // 2 * 2:2]
    slack = jnp.minimum(lengths[giver] - 1, most - lengths[receiver]) // 2
    slack = jnp.where((giver == order[0]) | (receiver == order[0]) | (lengths[receiver] == 0), 0, jnp.maximum(slack, 0))
    shifted = jax.random.randint(jax.random.fold_in(own, 4), (count // 2,), 0, 1 << 20) % (slack + 1)
    lengths = lengths.at[giver].add(-shifted).at[receiver].add(shifted)
    items = jnp.searchsorted(jnp.cumsum(lengths), jnp.arange(rows * top), side="right").astype(jnp.int32)
    listing = items.reshape(top, rows).T
    listing = listing[jax.random.permutation(jax.random.fold_in(own, 1), rows)]
    offset_by = jax.random.randint(jax.random.fold_in(own, 2), (rows, 1), 0, top)
    return jnp.take_along_axis(listing, (jnp.arange(top)[None, :] + offset_by) % top, axis=1)


def shares(count, total, reach, lean, full):
    weights = [(1 << 20) // math.isqrt(rank ** lean) + 1 for rank in range(1, count + 1)]
    largest = reach if full else min(reach, max(-(-total // count), total * weights[0] // sum(weights)))
    least = 1 if total - largest >= count - 1 else 0
    holding, rest = [largest] + [least] * (count - 1), total - largest - least * (count - 1)
    while rest > 0:
        candidates = [i for i in range(1, count) if holding[i] < largest] or [i for i in range(1, count) if holding[i] < reach]
        mass, left = sum([weights[i] for i in candidates]), rest
        for i in candidates:
            extra = min(reach - holding[i], max(1, left * weights[i] // mass), rest)
            holding[i] = holding[i] + extra
            rest = rest - extra
    return np.array(holding)


def normal_values(own_key, extent, deviation, most, pieces=(), kind=jnp.bfloat16):
    level = shard_levels(own_key, extent, pieces, -0.22, 0.18) if pieces else 1.0
    result = jax.random.normal(own_key, extent, jnp.float32) * deviation * level
    return jnp.minimum(jnp.maximum(result, -most), most).astype(kind)


def setup_inputs(seed: int = 0) -> dict:
    keys = jax.random.split(jax.random.key(seed), 8)
    tokens = normal_values(keys[0], (TOKENS, D), 1.0, 6.0, ((0, 8), (1, 4)))
    expert_ids_keys = jax.random.split(jax.random.fold_in(keys[1], 1), TOKENS // TOKENS)
    expert_ids_turns = jax.random.permutation(jax.random.fold_in(keys[1], 3), TOKENS // TOKENS)
    expert_ids = jax.vmap(lambda own, number: deal_out(jax.random.fold_in(keys[1], 2), own, number, TOKENS, EXPERTS, TOP, CAP, 2))(expert_ids_keys, expert_ids_turns).reshape((TOKENS, TOP))
    routing_weights = jnp.clip(0.049804688 + 0.24902344 * jax.random.uniform(keys[2], (TOKENS, TOP), jnp.float32) ** shard_levels(keys[2], (TOKENS, TOP), ((0, 8),), -0.2, 0.2), 0.049804688, 0.29882812).astype(jnp.bfloat16)
    gate_weight = normal_values(keys[3], (EXPERTS, FF, D), D ** -0.5, 0.09375, ((0, 8), (2, 4)))
    up_weight = normal_values(keys[4], (EXPERTS, FF, D), D ** -0.5, 0.09375, ((0, 8), (2, 4)))
    down_weight = normal_values(keys[5], (EXPERTS, FF, D), FF ** -0.5, 0.21875, ((0, 8), (2, 4)))
    out_grad = normal_values(keys[6], (TOKENS, D), 0.25, 1.5, ((0, 8), (1, 4)))
    return dict(tokens=tokens, expert_ids=expert_ids, routing_weights=routing_weights, gate_weight=gate_weight, up_weight=up_weight, down_weight=down_weight, out_grad=out_grad)


def build_lists(flat_ids, expert):
    matches = flat_ids == expert
    rank_pos = jnp.cumsum(matches.astype(jnp.int32), dtype=jnp.int32) - 1
    target_pos = jnp.where(matches, rank_pos, CAP).astype(jnp.int32)
    slot_ids = jnp.arange(flat_ids.shape[0], dtype=jnp.int32)
    slot_lists = jnp.zeros((CAP,), jnp.int32).at[target_pos].set(slot_ids, mode="drop")
    total = jnp.sum(matches.astype(jnp.int32), dtype=jnp.int32)
    is_live = jnp.arange(CAP, dtype=jnp.int32) < total
    return slot_lists, is_live


def grouped_sum(left, right):
    group_width = D // N_DP
    parts = jnp.einsum("rjd,fjd->jrf", left.reshape(CAP, N_DP, group_width).astype(jnp.float32),
                       right.reshape(right.shape[0], N_DP, group_width).astype(jnp.float32))
    parts = lax.optimization_barrier(parts.astype(jnp.bfloat16))
    return jnp.sum(parts.astype(jnp.float32), axis=0)


def reference(tokens, expert_ids, routing_weights, gate_weight, up_weight, down_weight, out_grad):
    flat_ids = expert_ids.reshape(-1)
    flat_weights = routing_weights.reshape(-1).astype(jnp.float32)
    group_width = D // N_DP

    def one_group(carry, inputs):
        out_sum, input_sum, weight_sum = carry
        group, gate_set, up_set, down_set = inputs
        group_out = jnp.zeros((TOKENS, D), jnp.float32)
        group_in = jnp.zeros((TOKENS, D), jnp.float32)
        gate_list, up_list, down_list = [], [], []
        for local in range(EXP_DEV):
            expert = (group * EXP_DEV + local).astype(jnp.int32)
            w_gate, w_up, w_down = gate_set[local], up_set[local], down_set[local]
            slot_lists, is_live = build_lists(flat_ids, expert)
            token_index = (slot_lists // TOP).astype(jnp.int32)
            live_rows = is_live.astype(jnp.float32)
            row_acts = jnp.where(is_live[:, None], tokens[token_index], jnp.zeros((), jnp.bfloat16))
            gate_pre = grouped_sum(row_acts, w_gate)
            up_pre = grouped_sum(row_acts, w_up)
            hidden = (jax.nn.silu(gate_pre) * up_pre).astype(jnp.bfloat16)
            expert_out = jnp.dot(hidden, w_down, preferred_element_type=jnp.float32)
            row_scale = flat_weights[slot_lists] * live_rows
            group_out = group_out.at[token_index].add(expert_out * row_scale[:, None])
            grad_rows = out_grad[token_index].astype(jnp.float32)
            dot_groups = jnp.sum((grad_rows * expert_out).reshape(CAP, N_DP, group_width), axis=2)
            dot_groups = lax.optimization_barrier(dot_groups.astype(jnp.bfloat16))
            dots = jnp.sum(dot_groups.astype(jnp.float32), axis=1) * live_rows
            weight_sum = weight_sum.at[slot_lists].add(dots)
            scaled_grad = (grad_rows * row_scale[:, None]).astype(jnp.bfloat16)
            hidden_grad = grouped_sum(scaled_grad, w_down)
            gate_sig = jax.nn.sigmoid(gate_pre)
            gate_delta = (hidden_grad * up_pre * gate_sig * (1.0 + gate_pre * (1.0 - gate_sig))).astype(jnp.bfloat16)
            up_delta = (hidden_grad * gate_pre * gate_sig).astype(jnp.bfloat16)
            down_list.append(jnp.dot(hidden.T, scaled_grad, preferred_element_type=jnp.float32).astype(jnp.bfloat16))
            gate_list.append(jnp.dot(gate_delta.T, row_acts, preferred_element_type=jnp.float32).astype(jnp.bfloat16))
            up_list.append(jnp.dot(up_delta.T, row_acts, preferred_element_type=jnp.float32).astype(jnp.bfloat16))
            row_grad = jnp.dot(gate_delta, w_gate, preferred_element_type=jnp.float32)
            row_grad = row_grad + jnp.dot(up_delta, w_up, preferred_element_type=jnp.float32)
            group_in = group_in.at[token_index].add(row_grad)
        out_sum = out_sum + lax.optimization_barrier(group_out.astype(jnp.bfloat16)).astype(jnp.float32)
        input_sum = input_sum + lax.optimization_barrier(group_in.astype(jnp.bfloat16)).astype(jnp.float32)
        return (out_sum, input_sum, weight_sum), (jnp.stack(gate_list), jnp.stack(up_list), jnp.stack(down_list))

    start = (jnp.zeros((TOKENS, D), jnp.float32), jnp.zeros((TOKENS, D), jnp.float32),
             jnp.zeros((TOKENS * TOP,), jnp.float32))
    groups_all = jnp.arange(N_EXPERT, dtype=jnp.int32)
    (out_sum, input_sum, weight_sum), (gate_grads, up_grads, down_grads) = lax.scan(
        one_group, start,
        (groups_all, gate_weight.reshape(N_EXPERT, EXP_DEV, FF, D), up_weight.reshape(N_EXPERT, EXP_DEV, FF, D),
         down_weight.reshape(N_EXPERT, EXP_DEV, FF, D)))
    return (out_sum.astype(jnp.bfloat16), input_sum.astype(jnp.bfloat16), weight_sum.reshape(TOKENS, TOP),
            gate_grads.reshape(EXPERTS, FF, D), up_grads.reshape(EXPERTS, FF, D), down_grads.reshape(EXPERTS, FF, D))
```

```python
import functools
import jax
import jax.numpy as jnp
from jax import lax
from jax.experimental import pallas as pl
from jax.experimental.pallas import tpu as pltpu
from jax.sharding import PartitionSpec as P

CAP = 240
F32 = jnp.float32
BF = jnp.bfloat16
VM = pl.BlockSpec(memory_space=pltpu.VMEM)


def factor(n):
    slow = 4 if n % 4 == 0 else n
    return slow, n // slow


def remote(src, dst, send, recv, where):
    return pltpu.make_async_remote_copy(
        src_ref=src, dst_ref=dst, send_sem=send, recv_sem=recv,
        device_id=where, device_id_type=pl.DeviceIdType.MESH,
    )


def greet(axis, n):
    me = lax.axis_index(axis)
    sem = pltpu.get_barrier_semaphore()
    for j in range(1, n):
        pl.semaphore_signal(sem, inc=1, device_id={axis: lax.rem(me + j, n)},
                            device_id_type=pl.DeviceIdType.MESH)
    pl.semaphore_wait(sem, n - 1)


def gather_kernel(n, *refs):
    k = 3
    ins, outs = refs[:k], refs[k:2 * k]
    up_s, up_r, dn_s, dn_r, side_s, side_r = refs[2 * k:]
    slow, fast = factor(n)
    me = lax.axis_index("expert")
    a, b = me // fast, lax.rem(me, fast)
    for i in range(k):
        outs[i][me] = ins[i][...]
    greet("expert", n)

    def hop(i, block, target, s_sem, r_sem, own):
        src = ins[i] if own else outs[i].at[block]
        return remote(src, outs[i].at[block], s_sem, r_sem, {"expert": target})

    def side(i, block, slot, j, own):
        return hop(i, block, a * fast + lax.rem(b + j, fast),
                   side_s.at[i, slot, j], side_r.at[i, slot, j], own)

    def up(i, s):
        return hop(i, (a - s) * fast + b, (a + 1) * fast + b, up_s.at[i, s], up_r.at[i, s], s == 0)

    def down(i, s):
        return hop(i, (a + s) * fast + b, (a - 1) * fast + b, dn_s.at[i, s], dn_r.at[i, s], s == 0)

    order = (2, 0, 1)
    for s in range(slow):
        if s > 0:
            for i in order:
                @pl.when(a - s >= 0)
                def _():
                    up(i, s - 1).wait_recv()

                @pl.when(a + s < slow)
                def _():
                    down(i, s - 1).wait_recv()
        if s < slow - 1:
            for i in order:
                @pl.when((a - s >= 0) & (a + 1 < slow))
                def _():
                    up(i, s).start()

                @pl.when((a + s < slow) & (a >= 1))
                def _():
                    down(i, s).start()
        for i in order:
            for j in range(1, fast):
                if s == 0:
                    side(i, me, 0, j, True).start()
                else:
                    @pl.when(a - s >= 0)
                    def _():
                        side(i, (a - s) * fast + b, s, j, False).start()

                    @pl.when(a + s < slow)
                    def _():
                        side(i, (a + s) * fast + b, slow - 1 + s, j, False).start()
    for i in order:
        for s in range(slow):
            if s < slow - 1:
                @pl.when((a - s >= 0) & (a + 1 < slow))
                def _():
                    up(i, s).wait_send()

                @pl.when((a + s < slow) & (a >= 1))
                def _():
                    down(i, s).wait_send()
            for j in range(1, fast):
                if s == 0:
                    side(i, me, 0, j, True).wait()
                else:
                    @pl.when(a - s >= 0)
                    def _():
                        side(i, (a - s) * fast + b, s, j, False).wait()

                    @pl.when(a + s < slow)
                    def _():
                        side(i, (a + s) * fast + b, slow - 1 + s, j, False).wait()


def gather_all(n, tok, grad, meta):
    ins = (tok, grad, meta)
    slow, fast = factor(n)
    dma = pltpu.SemaphoreType.DMA
    return pl.pallas_call(
        functools.partial(gather_kernel, n),
        out_shape=[jax.ShapeDtypeStruct((n,) + x.shape, x.dtype) for x in ins],
        in_specs=[VM] * 3,
        out_specs=[VM] * 3,
        scratch_shapes=[dma((3, slow))] * 4 + [dma((3, 2 * slow, fast))] * 2,
        compiler_params=pltpu.CompilerParams(collective_id=0, has_side_effects=True,
                                             vmem_limit_bytes=48 << 20),
    )(*ins)


def mix_kernel(n, ch, *refs):
    ins, outs = refs[:3], refs[3:6]
    got1, mine, got2, s1, r1, s2, r2, s3, r3, s4, r4 = refs[6:]
    m = n // 2
    me = lax.axis_index("dp")
    chip, core = me // 2, lax.rem(me, 2)
    greet("dp", n)
    partner = {"dp": chip * 2 + 1 - core}

    def pair(i, j, h):
        c = lax.rem(chip + j, m)
        seg = (c * 2 + 1 - core) * ch + h
        return remote(ins[i].at[seg], got1.at[i, j, h], s1.at[i, j, h], r1.at[i, j, h], partner)

    def cross(i, j, h):
        return remote(mine.at[i, j, h], got2.at[i, j, h], s2.at[i, j, h], r2.at[i, j, h],
                      {"dp": lax.rem(chip + j, m) * 2 + core})

    def spread(i, j, h):
        seg = me * ch + h
        return remote(outs[i].at[seg], outs[i].at[seg], s3.at[i, j, h], r3.at[i, j, h],
                      {"dp": lax.rem(chip + j, m) * 2 + core})

    def share(i, j, h):
        seg = (lax.rem(chip + m - j, m) * 2 + core) * ch + h
        return remote(outs[i].at[seg], outs[i].at[seg], s4.at[i, j, h], r4.at[i, j, h], partner)

    order = list(range(1, m)) + [0]
    for h in range(ch):
        for j in order:
            for i in range(3):
                pair(i, j, h).start()
    for h in range(ch):
        for j in order:
            for i in range(3):
                pair(i, j, h).wait_recv()
                seg = (lax.rem(chip + j, m) * 2 + core) * ch + h
                if j > 0:
                    mine[i, j, h] = (ins[i][seg].astype(F32) + got1[i, j, h].astype(F32)).astype(BF)
                    cross(i, j, h).start()
    for h in range(ch):
        total = []
        for i in range(3):
            v = ins[i][me * ch + h].astype(F32) + got1[i, 0, h].astype(F32)
            for j in range(1, m):
                cross(i, j, h).wait_recv()
                v = v + got2[i, j, h].astype(F32)
            total.append(v)
        gate, up, hg = total
        sig = jax.nn.sigmoid(gate)
        outs[0][me * ch + h] = (gate * sig * up).astype(BF)
        outs[1][me * ch + h] = (hg * up * sig * (1.0 + gate * (1.0 - sig))).astype(BF)
        outs[2][me * ch + h] = (hg * gate * sig).astype(BF)
        for i in range(3):
            for j in range(1, m):
                spread(i, j, h).start()
            share(i, 0, h).start()
    for h in range(ch):
        for j in range(1, m):
            for i in range(3):
                spread(i, j, h).wait_recv()
                share(i, j, h).start()
    for h in range(ch):
        for i in range(3):
            for j in range(m):
                pair(i, j, h).wait_send()
                share(i, j, h).wait()
                if j > 0:
                    cross(i, j, h).wait_send()
                    spread(i, j, h).wait_send()


def mix(n, gate, up, hg):
    rows, width = gate.shape
    ch = 3 if rows % (n * 3 * 8) == 0 else 1
    r = rows // (n * ch)
    ins = [x.reshape(n * ch, r, width) for x in (gate, up, hg)]
    m = n // 2
    dma = pltpu.SemaphoreType.DMA
    outs = pl.pallas_call(
        functools.partial(mix_kernel, n, ch),
        out_shape=[jax.ShapeDtypeStruct((n * ch, r, width), BF)] * 3,
        in_specs=[VM] * 3,
        out_specs=[VM] * 3,
        scratch_shapes=[pltpu.VMEM((3, m, ch, r, width), BF)] * 3 + [dma((3, m, ch))] * 8,
        compiler_params=pltpu.CompilerParams(collective_id=1, has_side_effects=True,
                                             vmem_limit_bytes=48 << 20),
    )(*ins)
    return [x.reshape(rows, width) for x in outs]


def reduce_kernel(n, nd, *refs):
    k = 3
    ins, outs = refs[:k], refs[k:2 * k]
    side_b, acc, up_b, dn_b, dots = refs[2 * k:3 * k], refs[3 * k:4 * k], refs[4 * k:5 * k], refs[5 * k:6 * k], refs[6 * k]
    side_s, side_r, up_s, up_r, dn_s, dn_r, dp_s, dp_r = refs[6 * k + 1:]
    slow, fast = factor(n)
    me = lax.axis_index("expert")
    dp = lax.axis_index("dp")
    a, b = me // fast, lax.rem(me, fast)
    sem = pltpu.get_barrier_semaphore()
    for j in range(1, n):
        pl.semaphore_signal(sem, inc=1, device_id={"expert": lax.rem(me + j, n)},
                            device_id_type=pl.DeviceIdType.MESH)
    for j in range(1, nd):
        pl.semaphore_signal(sem, inc=1, device_id={"dp": lax.rem(dp + j, nd)},
                            device_id_type=pl.DeviceIdType.MESH)
    pl.semaphore_wait(sem, n - 1 + nd - 1)

    def side(i, t, j):
        bb = lax.rem(b + j, fast)
        return remote(ins[i].at[t * fast + bb], side_b[i].at[t, j], side_s.at[i, t, j], side_r.at[i, t, j],
                      {"expert": a * fast + bb})

    def up(i, t):
        return remote(acc[i].at[t], up_b[i].at[t], up_s.at[i, t], up_r.at[i, t], {"expert": (a + 1) * fast + b})

    def down(i, t):
        return remote(acc[i].at[t], dn_b[i].at[t], dn_s.at[i, t], dn_r.at[i, t], {"expert": (a - 1) * fast + b})

    far = [t for d in range(slow) for t in ((slow - 1 - d, d) if slow - 1 - d > d else ((d,) if slow - 1 - d == d else ()))]
    for t in far:
        for i in range(k):
            for j in range(1, fast):
                side(i, t, j).start()
    for t in far:
        for i in range(k):
            v = ins[i][t * fast + b].astype(F32)
            for j in range(1, fast):
                side(i, t, j).wait_recv()
                v = v + side_b[i][t, j].astype(F32)
            acc[i][t] = v.astype(acc[i].dtype)

            @pl.when((t > a) & (a > 0))
            def _():
                up(i, t).wait_recv()
                acc[i][t] = (acc[i][t].astype(F32) + up_b[i][t].astype(F32)).astype(acc[i].dtype)

            @pl.when(t > a)
            def _():
                up(i, t).start()

            @pl.when((t < a) & (a < slow - 1))
            def _():
                down(i, t).wait_recv()
                acc[i][t] = (acc[i][t].astype(F32) + dn_b[i][t].astype(F32)).astype(acc[i].dtype)

            @pl.when(t < a)
            def _():
                down(i, t).start()

    def across(j):
        return remote(dots.at[0], dots.at[j], dp_s.at[j], dp_r.at[j], {"dp": lax.rem(dp + j, nd)})

    for i in (2, 0, 1):
        @pl.when(a > 0)
        def _():
            up(i, a).wait_recv()
            acc[i][a] = (acc[i][a].astype(F32) + up_b[i][a].astype(F32)).astype(acc[i].dtype)

        @pl.when(a < slow - 1)
        def _():
            down(i, a).wait_recv()
            acc[i][a] = (acc[i][a].astype(F32) + dn_b[i][a].astype(F32)).astype(acc[i].dtype)

        if i == 2:
            dots[0] = acc[2][a]
            for j in range(1, nd):
                across(j).start()
        else:
            outs[i][...] = acc[i][a]
    v = dots[0]
    for j in range(1, nd):
        across(j).wait()
        v = v + dots[j]
    outs[2][...] = v
    for t in range(slow):
        for i in range(k):
            for j in range(1, fast):
                side(i, t, j).wait_send()

            @pl.when(t > a)
            def _():
                up(i, t).wait_send()

            @pl.when(t < a)
            def _():
                down(i, t).wait_send()


def reduce_all(n, nd, out_rows, in_rows, dot_rows):
    ins = [x.reshape(n, x.shape[0] // n, x.shape[1]) for x in (out_rows, in_rows, dot_rows)]
    slow, fast = factor(n)
    dma = pltpu.SemaphoreType.DMA
    blocks = [(x.shape[1:], x.dtype) for x in ins]
    return pl.pallas_call(
        functools.partial(reduce_kernel, n, nd),
        out_shape=[jax.ShapeDtypeStruct(s, d) for s, d in blocks],
        in_specs=[VM] * 3,
        out_specs=[VM] * 3,
        scratch_shapes=[pltpu.VMEM((slow, fast) + s, d) for s, d in blocks]
        + [pltpu.VMEM((slow,) + s, d) for s, d in blocks] * 3
        + [pltpu.VMEM((nd,) + blocks[2][0], blocks[2][1])]
        + [dma((3, slow, fast))] * 2 + [dma((3, slow))] * 4 + [dma((nd,))] * 2,
        compiler_params=pltpu.CompilerParams(collective_id=2, has_side_effects=True,
                                             vmem_limit_bytes=48 << 20),
    )(*ins)


def body(n, nd, tokens, expert_ids, routing_weights, gate_weight, up_weight, down_weight, out_grad):
    e, f, d = gate_weight.shape
    top = expert_ids.shape[1]
    meta = jnp.concatenate([expert_ids.astype(F32), routing_weights.astype(F32)], axis=1)
    meta = jnp.pad(meta, ((0, 0), (0, 128 - 2 * top)))
    tok, grad, meta = gather_all(n, tokens, out_grad, meta)
    tok, grad = tok.reshape(-1, d), grad.reshape(-1, d)
    meta = meta.reshape(-1, 128)
    t = tok.shape[0]
    first = lax.axis_index("expert") * e
    targets = (first + jnp.arange(e, dtype=jnp.int32)).astype(F32)
    hit = meta[None, :, :top] == targets[:, None, None]
    match = jnp.any(hit, axis=2)
    weight = jnp.sum(jnp.where(hit, meta[None, :, top:2 * top], 0.0), axis=2)
    lower = (jnp.arange(t)[:, None] < jnp.arange(t)[None, :]).astype(BF)
    rank = jnp.dot(match.astype(BF), lower, preferred_element_type=F32).astype(jnp.int32)
    place = jnp.where(match, rank, CAP)
    pick = place[:, None, :] == jnp.arange(CAP, dtype=jnp.int32)[None, :, None]
    one = pick.astype(BF).reshape(e * CAP, t)
    scaled = jnp.where(pick, weight[:, None, :], 0.0).astype(BF).reshape(e * CAP, t)
    rows = jnp.dot(one, tok, preferred_element_type=F32).astype(BF).reshape(e, CAP, d)
    grows = jnp.dot(one, grad, preferred_element_type=F32).reshape(e, CAP, d)
    sgrad = jnp.dot(scaled, grad, preferred_element_type=F32).astype(BF).reshape(e, CAP, d)

    def ein(s, x, y):
        return jnp.einsum(s, x, y, preferred_element_type=F32)

    gate_part = ein("ecd,efd->ecf", rows, gate_weight).astype(BF).reshape(e * CAP, f)
    up_part = ein("ecd,efd->ecf", rows, up_weight).astype(BF).reshape(e * CAP, f)
    hg_part = ein("ecd,efd->ecf", sgrad, down_weight).astype(BF).reshape(e * CAP, f)
    hidden, gd, ud = [x.reshape(e, CAP, f) for x in mix(nd, gate_part, up_part, hg_part)]
    eo = ein("ecf,efd->ecd", hidden, down_weight)
    dots = jnp.sum(grows * eo, axis=2).astype(BF)
    dot_te = jnp.einsum("ect,ec->et", one.reshape(e, CAP, t), dots, preferred_element_type=F32)
    dot_rows = jnp.sum(jnp.where(hit, dot_te[:, :, None], 0.0), axis=0)
    dot_rows = jnp.pad(dot_rows, ((0, 0), (0, 128 - top)))
    out_rows = jnp.einsum("rt,rd->td", scaled, eo.reshape(e * CAP, d).astype(BF), preferred_element_type=F32).astype(BF)
    terms = (ein("ecf,efd->ecd", gd, gate_weight) + ein("ecf,efd->ecd", ud, up_weight)).astype(BF)
    in_rows = jnp.einsum("rt,rd->td", one, terms.reshape(e * CAP, d), preferred_element_type=F32).astype(BF)
    layer_out, tokens_grad, routing_grad = reduce_all(n, nd, out_rows, in_rows, dot_rows)
    down_grad = ein("ecf,ecd->efd", hidden, sgrad).astype(BF)
    gate_grad = ein("ecf,ecd->efd", gd, rows).astype(BF)
    up_grad = ein("ecf,ecd->efd", ud, rows).astype(BF)
    return layer_out, tokens_grad, routing_grad[:, :top], gate_grad, up_grad, down_grad


def solution(mesh):
    n, nd = mesh.shape["expert"], mesh.shape["dp"]
    w = P("expert", None, "dp")
    x = P("expert", "dp")
    r = P("expert", None)
    return jax.shard_map(functools.partial(body, n, nd), mesh=mesh, in_specs=(x, r, r, w, w, w, x),
                         out_specs=(x, x, r, w, w, w), check_vma=False)
```

```python
import functools
import jax
import jax.numpy as jnp
from jax import lax
from jax.experimental import pallas as pl
from jax.experimental.pallas import tpu as pltpu
from jax.sharding import PartitionSpec as P

CAP = 240
F32 = jnp.float32
BF = jnp.bfloat16
VM = pl.BlockSpec(memory_space=pltpu.VMEM)


def factor(n):
    slow = 4 if n % 4 == 0 else n
    return slow, n // slow


def remote(src, dst, send, recv, where):
    return pltpu.make_async_remote_copy(
        src_ref=src, dst_ref=dst, send_sem=send, recv_sem=recv,
        device_id=where, device_id_type=pl.DeviceIdType.MESH,
    )


def greet(axis, n):
    me = lax.axis_index(axis)
    sem = pltpu.get_barrier_semaphore()
    for j in range(1, n):
        pl.semaphore_signal(sem, inc=1, device_id={axis: lax.rem(me + j, n)},
                            device_id_type=pl.DeviceIdType.MESH)
    pl.semaphore_wait(sem, n - 1)


def gather_kernel(n, *refs):
    k = 3
    ins, outs = refs[:k], refs[k:2 * k]
    up_s, up_r, dn_s, dn_r, side_s, side_r = refs[2 * k:]
    slow, fast = factor(n)
    me = lax.axis_index("expert")
    a, b = me // fast, lax.rem(me, fast)
    for i in range(k):
        outs[i][me] = ins[i][...]
    greet("expert", n)

    def hop(i, block, target, s_sem, r_sem, own):
        src = ins[i] if own else outs[i].at[block]
        return remote(src, outs[i].at[block], s_sem, r_sem, {"expert": target})

    def side(i, block, slot, j, own):
        return hop(i, block, a * fast + lax.rem(b + j, fast),
                   side_s.at[i, slot, j], side_r.at[i, slot, j], own)

    def up(i, s):
        return hop(i, (a - s) * fast + b, (a + 1) * fast + b, up_s.at[i, s], up_r.at[i, s], s == 0)

    def down(i, s):
        return hop(i, (a + s) * fast + b, (a - 1) * fast + b, dn_s.at[i, s], dn_r.at[i, s], s == 0)

    order = (2, 0, 1)
    for s in range(slow):
        if s > 0:
            for i in order:
                @pl.when(a - s >= 0)
                def _():
                    up(i, s - 1).wait_recv()

                @pl.when(a + s < slow)
                def _():
                    down(i, s - 1).wait_recv()
        if s < slow - 1:
            for i in order:
                @pl.when((a - s >= 0) & (a + 1 < slow))
                def _():
                    up(i, s).start()

                @pl.when((a + s < slow) & (a >= 1))
                def _():
                    down(i, s).start()
        for i in order:
            for j in range(1, fast):
                if s == 0:
                    side(i, me, 0, j, True).start()
                else:
                    @pl.when(a - s >= 0)
                    def _():
                        side(i, (a - s) * fast + b, s, j, False).start()

                    @pl.when(a + s < slow)
                    def _():
                        side(i, (a + s) * fast + b, slow - 1 + s, j, False).start()
    for i in order:
        for s in range(slow):
            if s < slow - 1:
                @pl.when((a - s >= 0) & (a + 1 < slow))
                def _():
                    up(i, s).wait_send()

                @pl.when((a + s < slow) & (a >= 1))
                def _():
                    down(i, s).wait_send()
            for j in range(1, fast):
                if s == 0:
                    side(i, me, 0, j, True).wait()
                else:
                    @pl.when(a - s >= 0)
                    def _():
                        side(i, (a - s) * fast + b, s, j, False).wait()

                    @pl.when(a + s < slow)
                    def _():
                        side(i, (a + s) * fast + b, slow - 1 + s, j, False).wait()


def gather_all(n, tok, grad, meta):
    ins = (tok, grad, meta)
    slow, fast = factor(n)
    dma = pltpu.SemaphoreType.DMA
    return pl.pallas_call(
        functools.partial(gather_kernel, n),
        out_shape=[jax.ShapeDtypeStruct((n,) + x.shape, x.dtype) for x in ins],
        in_specs=[VM] * 3,
        out_specs=[VM] * 3,
        scratch_shapes=[dma((3, slow))] * 4 + [dma((3, 2 * slow, fast))] * 2,
        compiler_params=pltpu.CompilerParams(collective_id=0, has_side_effects=True,
                                             vmem_limit_bytes=48 << 20),
    )(*ins)


def mix_kernel(n, ch, *refs):
    ins, outs = refs[:3], refs[3:6]
    got1, mine, got2, s1, r1, s2, r2, s3, r3, s4, r4 = refs[6:]
    m = n // 2
    me = lax.axis_index("dp")
    chip, core = me // 2, lax.rem(me, 2)
    greet("dp", n)
    partner = {"dp": chip * 2 + 1 - core}

    def pair(i, j, h):
        c = lax.rem(chip + j, m)
        seg = (c * 2 + 1 - core) * ch + h
        return remote(ins[i].at[seg], got1.at[i, j, h], s1.at[i, j, h], r1.at[i, j, h], partner)

    def cross(i, j, h):
        return remote(mine.at[i, j, h], got2.at[i, j, h], s2.at[i, j, h], r2.at[i, j, h],
                      {"dp": lax.rem(chip + j, m) * 2 + core})

    def spread(i, j, h):
        seg = me * ch + h
        return remote(outs[i].at[seg], outs[i].at[seg], s3.at[i, j, h], r3.at[i, j, h],
                      {"dp": lax.rem(chip + j, m) * 2 + core})

    def share(i, j, h):
        seg = (lax.rem(chip + m - j, m) * 2 + core) * ch + h
        return remote(outs[i].at[seg], outs[i].at[seg], s4.at[i, j, h], r4.at[i, j, h], partner)

    order = list(range(1, m)) + [0]
    for h in range(ch):
        for j in order:
            for i in range(3):
                pair(i, j, h).start()
    for h in range(ch):
        for j in order:
            for i in range(3):
                pair(i, j, h).wait_recv()
                seg = (lax.rem(chip + j, m) * 2 + core) * ch + h
                if j > 0:
                    mine[i, j, h] = (ins[i][seg].astype(F32) + got1[i, j, h].astype(F32)).astype(BF)
                    cross(i, j, h).start()
    for h in range(ch):
        total = []
        for i in range(3):
            v = ins[i][me * ch + h].astype(F32) + got1[i, 0, h].astype(F32)
            for j in range(1, m):
                cross(i, j, h).wait_recv()
                v = v + got2[i, j, h].astype(F32)
            total.append(v)
        gate, up, hg = total
        sig = jax.nn.sigmoid(gate)
        outs[0][me * ch + h] = (gate * sig * up).astype(BF)
        outs[1][me * ch + h] = (hg * up * sig * (1.0 + gate * (1.0 - sig))).astype(BF)
        outs[2][me * ch + h] = (hg * gate * sig).astype(BF)
        for i in range(3):
            for j in range(1, m):
                spread(i, j, h).start()
            share(i, 0, h).start()
    for h in range(ch):
        for j in range(1, m):
            for i in range(3):
                spread(i, j, h).wait_recv()
                share(i, j, h).start()
    for h in range(ch):
        for i in range(3):
            for j in range(m):
                pair(i, j, h).wait_send()
                share(i, j, h).wait()
                if j > 0:
                    cross(i, j, h).wait_send()
                    spread(i, j, h).wait_send()


def mix(n, gate, up, hg):
    rows, width = gate.shape
    ch = 3 if rows % (n * 3 * 8) == 0 else 1
    r = rows // (n * ch)
    ins = [x.reshape(n * ch, r, width) for x in (gate, up, hg)]
    m = n // 2
    dma = pltpu.SemaphoreType.DMA
    outs = pl.pallas_call(
        functools.partial(mix_kernel, n, ch),
        out_shape=[jax.ShapeDtypeStruct((n * ch, r, width), BF)] * 3,
        in_specs=[VM] * 3,
        out_specs=[VM] * 3,
        scratch_shapes=[pltpu.VMEM((3, m, ch, r, width), BF)] * 3 + [dma((3, m, ch))] * 8,
        compiler_params=pltpu.CompilerParams(collective_id=1, has_side_effects=True,
                                             vmem_limit_bytes=48 << 20),
    )(*ins)
    return [x.reshape(rows, width) for x in outs]


def reduce_kernel(n, nd, *refs):
    k = 3
    ins, outs = refs[:k], refs[k:2 * k]
    side_b, acc, up_b, dn_b, dots = refs[2 * k:3 * k], refs[3 * k:4 * k], refs[4 * k:5 * k], refs[5 * k:6 * k], refs[6 * k]
    side_s, side_r, up_s, up_r, dn_s, dn_r, dp_s, dp_r = refs[6 * k + 1:]
    slow, fast = factor(n)
    me = lax.axis_index("expert")
    dp = lax.axis_index("dp")
    a, b = me // fast, lax.rem(me, fast)
    sem = pltpu.get_barrier_semaphore()
    for j in range(1, n):
        pl.semaphore_signal(sem, inc=1, device_id={"expert": lax.rem(me + j, n)},
                            device_id_type=pl.DeviceIdType.MESH)
    for j in range(1, nd):
        pl.semaphore_signal(sem, inc=1, device_id={"dp": lax.rem(dp + j, nd)},
                            device_id_type=pl.DeviceIdType.MESH)
    pl.semaphore_wait(sem, n - 1 + nd - 1)

    def side(i, t, j):
        bb = lax.rem(b + j, fast)
        return remote(ins[i].at[t * fast + bb], side_b[i].at[t, j], side_s.at[i, t, j], side_r.at[i, t, j],
                      {"expert": a * fast + bb})

    def up(i, t):
        return remote(acc[i].at[t], up_b[i].at[t], up_s.at[i, t], up_r.at[i, t], {"expert": (a + 1) * fast + b})

    def down(i, t):
        return remote(acc[i].at[t], dn_b[i].at[t], dn_s.at[i, t], dn_r.at[i, t], {"expert": (a - 1) * fast + b})

    far = [t for d in range(slow) for t in ((slow - 1 - d, d) if slow - 1 - d > d else ((d,) if slow - 1 - d == d else ()))]
    for t in far:
        for i in range(k):
            for j in range(1, fast):
                side(i, t, j).start()
    for t in far:
        for i in range(k):
            v = ins[i][t * fast + b].astype(F32)
            for j in range(1, fast):
                side(i, t, j).wait_recv()
                v = v + side_b[i][t, j].astype(F32)
            acc[i][t] = v.astype(acc[i].dtype)

            @pl.when((t > a) & (a > 0))
            def _():
                up(i, t).wait_recv()
                acc[i][t] = (acc[i][t].astype(F32) + up_b[i][t].astype(F32)).astype(acc[i].dtype)

            @pl.when(t > a)
            def _():
                up(i, t).start()

            @pl.when((t < a) & (a < slow - 1))
            def _():
                down(i, t).wait_recv()
                acc[i][t] = (acc[i][t].astype(F32) + dn_b[i][t].astype(F32)).astype(acc[i].dtype)

            @pl.when(t < a)
            def _():
                down(i, t).start()

    def across(j):
        return remote(dots.at[0], dots.at[j], dp_s.at[j], dp_r.at[j], {"dp": lax.rem(dp + j, nd)})

    for i in (2, 0, 1):
        @pl.when(a > 0)
        def _():
            up(i, a).wait_recv()
            acc[i][a] = (acc[i][a].astype(F32) + up_b[i][a].astype(F32)).astype(acc[i].dtype)

        @pl.when(a < slow - 1)
        def _():
            down(i, a).wait_recv()
            acc[i][a] = (acc[i][a].astype(F32) + dn_b[i][a].astype(F32)).astype(acc[i].dtype)

        if i == 2:
            dots[0] = acc[2][a]
            for j in range(1, nd):
                across(j).start()
        else:
            outs[i][...] = acc[i][a]
    v = dots[0]
    for j in range(1, nd):
        across(j).wait()
        v = v + dots[j]
    outs[2][...] = v
    for t in range(slow):
        for i in range(k):
            for j in range(1, fast):
                side(i, t, j).wait_send()

            @pl.when(t > a)
            def _():
                up(i, t).wait_send()

            @pl.when(t < a)
            def _():
                down(i, t).wait_send()


def reduce_all(n, nd, out_rows, in_rows, dot_rows):
    ins = [x.reshape(n, x.shape[0] // n, x.shape[1]) for x in (out_rows, in_rows, dot_rows)]
    slow, fast = factor(n)
    dma = pltpu.SemaphoreType.DMA
    blocks = [(x.shape[1:], x.dtype) for x in ins]
    return pl.pallas_call(
        functools.partial(reduce_kernel, n, nd),
        out_shape=[jax.ShapeDtypeStruct(s, d) for s, d in blocks],
        in_specs=[VM] * 3,
        out_specs=[VM] * 3,
        scratch_shapes=[pltpu.VMEM((slow, fast) + s, d) for s, d in blocks]
        + [pltpu.VMEM((slow,) + s, d) for s, d in blocks] * 3
        + [pltpu.VMEM((nd,) + blocks[2][0], blocks[2][1])]
        + [dma((3, slow, fast))] * 2 + [dma((3, slow))] * 4 + [dma((nd,))] * 2,
        compiler_params=pltpu.CompilerParams(collective_id=2, has_side_effects=True,
                                             vmem_limit_bytes=48 << 20),
    )(*ins)


def dotted(x, y, dx, dy):
    return lax.dot_general(x, y, (((dx,), (dy,)), ((), ())), preferred_element_type=F32)


def rows_kernel(e, match_ref, weight_ref, tok_ref, grad_ref, one_ref, scaled_ref, rows_ref, grows_ref, sgrad_ref):
    t = tok_ref.shape[0]
    lower = (lax.broadcasted_iota(jnp.int32, (t, t), 0) < lax.broadcasted_iota(jnp.int32, (t, t), 1)).astype(F32)
    match = match_ref[...]
    rank = dotted(match.astype(BF), lower.astype(BF), 1, 0)
    place = jnp.where(match > 0.5, rank, -1.0)
    line = lax.broadcasted_iota(jnp.int32, (CAP, t), 0).astype(F32)
    for i in range(e):
        pick = jnp.abs(line - place[i:i + 1, :]) < 0.5
        one = jnp.where(pick, 1.0, 0.0).astype(BF)
        scaled = jnp.where(pick, weight_ref[i:i + 1, :], 0.0).astype(BF)
        one_ref[i] = one
        scaled_ref[i] = scaled
        rows_ref[i] = dotted(one, tok_ref[...], 1, 0).astype(BF)
        grows_ref[i] = dotted(one, grad_ref[...], 1, 0).astype(BF)
        sgrad_ref[i] = dotted(scaled, grad_ref[...], 1, 0).astype(BF)


def make_rows(match, weight, tok, grad):
    e, t = match.shape
    d = tok.shape[1]
    pad = ((0, 16 - e), (0, 0))
    pick = jax.ShapeDtypeStruct((e, CAP, t), BF)
    wide = jax.ShapeDtypeStruct((e, CAP, d), BF)
    return pl.pallas_call(
        functools.partial(rows_kernel, e), out_shape=[pick, pick, wide, wide, wide],
        in_specs=[VM] * 4, out_specs=[VM] * 5,
        compiler_params=pltpu.CompilerParams(vmem_limit_bytes=48 << 20),
    )(jnp.pad(match.astype(F32), pad), jnp.pad(weight, pad), tok, grad)


def weight_kernel(hid, gd, ud, rows, sgrad, gate_o, up_o, down_o):
    gate_o[0] = dotted(gd[0], rows[0], 0, 0).astype(BF)
    up_o[0] = dotted(ud[0], rows[0], 0, 0).astype(BF)
    down_o[0] = dotted(hid[0], sgrad[0], 0, 0).astype(BF)


def weight_grads(hidden, gd, ud, rows, sgrad):
    e, c, f = hidden.shape
    d = rows.shape[2]
    fb = 256 if f % 256 == 0 else f
    narrow = pl.BlockSpec((1, c, fb), lambda i, j: (i, 0, j))
    whole = pl.BlockSpec((1, c, d), lambda i, j: (i, 0, 0))
    out = pl.BlockSpec((1, fb, d), lambda i, j: (i, j, 0))
    return pl.pallas_call(
        weight_kernel, grid=(e, f // fb), out_shape=[jax.ShapeDtypeStruct((e, f, d), BF)] * 3,
        in_specs=[narrow] * 3 + [whole] * 2, out_specs=[out] * 3,
        compiler_params=pltpu.CompilerParams(vmem_limit_bytes=48 << 20),
    )(hidden, gd, ud, rows, sgrad)


def back_kernel(e, gd, ud, gw, uw, one, out):
    total = None
    for i in range(e):
        terms = (dotted(gd[i], gw[i], 1, 0) + dotted(ud[i], uw[i], 1, 0)).astype(BF)
        part = dotted(one[i], terms, 0, 0)
        total = part if total is None else total + part
    out[...] = total.astype(BF)


def back_rows(gd, ud, gate_weight, up_weight, one):
    e, f, d = gate_weight.shape
    t = one.shape[2]
    db = 256 if d % 256 == 0 else d
    delta = pl.BlockSpec(gd.shape, lambda j: (0, 0, 0))
    w = pl.BlockSpec((e, f, db), lambda j: (0, 0, j))
    return pl.pallas_call(
        functools.partial(back_kernel, e), grid=(d // db,), out_shape=jax.ShapeDtypeStruct((t, d), BF),
        in_specs=[delta, delta, w, w, pl.BlockSpec(one.shape, lambda j: (0, 0, 0))],
        out_specs=pl.BlockSpec((t, db), lambda j: (0, j)),
        compiler_params=pltpu.CompilerParams(vmem_limit_bytes=48 << 20),
    )(gd, ud, gate_weight, up_weight, one)


def body(n, nd, tokens, expert_ids, routing_weights, gate_weight, up_weight, down_weight, out_grad):
    e, f, d = gate_weight.shape
    top = expert_ids.shape[1]
    meta = jnp.concatenate([expert_ids.astype(F32), routing_weights.astype(F32)], axis=1)
    meta = jnp.pad(meta, ((0, 0), (0, 128 - 2 * top)))
    tok, grad, meta = gather_all(n, tokens, out_grad, meta)
    tok, grad = tok.reshape(-1, d), grad.reshape(-1, d)
    meta = meta.reshape(-1, 128)
    t = tok.shape[0]
    first = lax.axis_index("expert") * e
    targets = (first + jnp.arange(e, dtype=jnp.int32)).astype(F32)
    hit = meta[None, :, :top] == targets[:, None, None]
    match = jnp.any(hit, axis=2)
    weight = jnp.sum(jnp.where(hit, meta[None, :, top:2 * top], 0.0), axis=2)
    one, scaled, rows, grows, sgrad = make_rows(match, weight, tok, grad)

    def ein(s, x, y):
        return jnp.einsum(s, x, y, preferred_element_type=F32)

    gate_part = ein("ecd,efd->ecf", rows, gate_weight).astype(BF).reshape(e * CAP, f)
    up_part = ein("ecd,efd->ecf", rows, up_weight).astype(BF).reshape(e * CAP, f)
    hg_part = ein("ecd,efd->ecf", sgrad, down_weight).astype(BF).reshape(e * CAP, f)
    hidden, gd, ud = [x.reshape(e, CAP, f) for x in mix(nd, gate_part, up_part, hg_part)]
    eo = ein("ecf,efd->ecd", hidden, down_weight)
    dots = jnp.sum(grows.astype(F32) * eo, axis=2).astype(BF)
    dot_te = jnp.einsum("ect,ec->et", one, dots, preferred_element_type=F32)
    dot_rows = jnp.sum(jnp.where(hit, dot_te[:, :, None], 0.0), axis=0)
    dot_rows = jnp.pad(dot_rows, ((0, 0), (0, 128 - top)))
    out_rows = jnp.einsum("rt,rd->td", scaled.reshape(e * CAP, t), eo.reshape(e * CAP, d).astype(BF), preferred_element_type=F32).astype(BF)
    in_rows = back_rows(gd, ud, gate_weight, up_weight, one)
    layer_out, tokens_grad, routing_grad = reduce_all(n, nd, out_rows, in_rows, dot_rows)
    gate_grad, up_grad, down_grad = weight_grads(hidden, gd, ud, rows, sgrad)
    return layer_out, tokens_grad, routing_grad[:, :top], gate_grad, up_grad, down_grad


def solution(mesh):
    n, nd = mesh.shape["expert"], mesh.shape["dp"]
    w = P("expert", None, "dp")
    x = P("expert", "dp")
    r = P("expert", None)
    return jax.shard_map(functools.partial(body, n, nd), mesh=mesh, in_specs=(x, r, r, w, w, w, x),
                         out_specs=(x, x, r, w, w, w), check_vma=False)
```
